32 devices in a mesh: oct: 2 (over x), space: 16 (over z, y, core).
Axes of the slice: x: 2, y: 2, z: 4, core: 2. Of those that a mesh axis runs over, the one named last changes fastest.
Arguments:
- distribution: float32 [1000, 96, 128], P('oct', 'space'), may hold values from 0.05 to 1
- collision_scale: float32 [1, 96, 128], P(None, 'space'), may hold values from 0.4 to 2.5
Outputs:
- advanced: float32 [1000, 96, 128], P('oct', 'space')
The draws below stay inside these ranges and needn't reach their ends.
All inputs are finite; a program needn't handle non-finite values.
Results may differ from the reference program's by a relative error of at most 0.0003.
Values sent between devices are 32-bit elements; how exact they have to be, the bound alone decides.
No kernel may reach another device: no remote copies, remote signals or barrier semaphores. Data moves between devices by JAX's collectives and lax.ppermute only.
A program may use at most 64 MiB of HBM per device.

```python
import math
import jax
import jax.numpy as jnp
from jax import lax

NV = 10
NZ = 16
STEPS = 3
VEL = 1000
NX = 96
PLANE = 128


def block_levels(own_key, extent, pieces, low, largest):
    gain = 1.0
    for dim, blocks in pieces:
        draws = jax.random.uniform(jax.random.fold_in(jax.random.fold_in(own_key, 6), dim), (blocks,), jnp.float32, low / len(pieces), largest / len(pieces))
        gain = gain * jnp.repeat(jnp.exp(draws), extent[dim] // blocks).reshape((-1,) + (1,) * (len(extent) - 1 - dim))
    return gain


def setup_inputs(seed: int = 0) -> dict:
    key_of = jax.random.split(jax.random.key(seed), 3)
    return {
        "distribution": jnp.clip(jnp.exp(math.log(1.0) - 2.9957323 * jax.random.uniform(key_of[0], (VEL, NX, PLANE), jnp.float32) ** block_levels(key_of[0], (VEL, NX, PLANE), ((0, 2), (1, 16)), -0.2, 0.2)), 0.05, 1.0),
        "collision_scale": jnp.clip(jnp.exp(math.log(2.5) - 1.8325814 * jax.random.uniform(key_of[1], (1, NX, PLANE), jnp.float32) ** block_levels(key_of[1], (1, NX, PLANE), ((1, 16),), -0.2, 0.2)), 0.4, 2.5),
    }


vel_bound = 4.0
courant = 0.08
time_step = 0.08
base_rate = 0.25
visc_index = 0.81
limiter_eps = 0.01


def velocity_parts(vel_index):
    half_count = NV // 2
    per_octant = half_count ** 3
    octant = vel_index // per_octant
    within = vel_index % per_octant
    spacing = 2.0 * vel_bound / NV
    sign_x = 1.0 - 2.0 * ((octant // 4) % 2).astype(jnp.float32)
    sign_y = 1.0 - 2.0 * ((octant // 2) % 2).astype(jnp.float32)
    sign_z = 1.0 - 2.0 * (octant % 2).astype(jnp.float32)
    vel_x = sign_x * ((within // (half_count * half_count)).astype(jnp.float32) + 0.5) * spacing
    vel_y = sign_y * (((within // half_count) % half_count).astype(jnp.float32) + 0.5) * spacing
    vel_z = sign_z * ((within % half_count).astype(jnp.float32) + 0.5) * spacing
    return vel_x, vel_y, vel_z


def moment_weights(vel_x, vel_y, vel_z):
    spacing = 2.0 * vel_bound / NV
    quad = spacing ** 3 * (2.0 * math.pi) ** -1.5
    rows = [jnp.ones_like(vel_x), vel_x, vel_y, vel_z, vel_x * vel_x + vel_y * vel_y + vel_z * vel_z]
    return quad * jnp.stack(rows)


def limited(left, right):
    return left * right * (left + right) / (left * left + right * right + limiter_eps)


def divergence_periodic(field, velocity, forward, backward):
    field_next = forward(field)
    slope = limited(field - backward(field), field_next - field)
    flux = jnp.maximum(velocity, 0.0) * (field + 0.5 * slope) + jnp.minimum(velocity, 0.0) * (field_next - 0.5 * forward(slope))
    return flux - backward(flux)


def y_forward(field):
    return jnp.roll(field, -NZ, axis=-1)


def y_backward(field):
    return jnp.roll(field, NZ, axis=-1)


def z_forward(field):
    z_place = lax.iota(jnp.int32, field.shape[-1]) % NZ
    return jnp.where(z_place == NZ - 1, jnp.roll(field, NZ - 1, axis=-1), jnp.roll(field, -1, axis=-1))


def z_backward(field):
    z_place = lax.iota(jnp.int32, field.shape[-1]) % NZ
    return jnp.where(z_place == 0, jnp.roll(field, 1 - NZ, axis=-1), jnp.roll(field, 1, axis=-1))


def x_forward(field):
    return jnp.roll(field, -1, axis=1)


def x_backward(field):
    return jnp.roll(field, 1, axis=1)


def relax(field, moments, rate_scale, vel_x, vel_y, vel_z):
    moments = moments.reshape(5, 1, field.shape[1], field.shape[2])
    density = moments[0]
    flow_x = moments[1] / density
    flow_y = moments[2] / density
    flow_z = moments[3] / density
    temper = (moments[4] / density - (flow_x * flow_x + flow_y * flow_y + flow_z * flow_z)) / 3.0
    rate = base_rate * rate_scale * density * temper ** (1.0 - visc_index)
    square = (vel_x - flow_x) ** 2 + (vel_y - flow_y) ** 2 + (vel_z - flow_z) ** 2
    equil = density * temper ** (-1.5) * jnp.exp(-square / (2.0 * temper))
    return time_step * rate * (equil - field)


def reference(distribution, collision_scale):
    groups = 8
    per_group = VEL // groups
    weights = moment_weights(*velocity_parts(lax.iota(jnp.int32, VEL)))
    field = distribution
    for step_id in range(STEPS):
        moments = jnp.dot(weights, field.reshape(VEL, -1), precision=lax.Precision.HIGHEST)

        def advance_group(pair):
            piece, group_id = pair
            vel_index = group_id * per_group + lax.iota(jnp.int32, per_group)
            vel_x, vel_y, vel_z = [parts[:, None, None] for parts in velocity_parts(vel_index)]
            change = divergence_periodic(piece, vel_x, x_forward, x_backward)
            change = change + divergence_periodic(piece, vel_y, y_forward, y_backward)
            change = change + divergence_periodic(piece, vel_z, z_forward, z_backward)
            return piece - courant * change + relax(piece, moments, collision_scale, vel_x, vel_y, vel_z)

        stacked = field.reshape(groups, per_group, NX, PLANE)
        field = lax.map(advance_group, (stacked, jnp.arange(groups, dtype=jnp.int32))).reshape(VEL, NX, PLANE)
    return field
```

```python
import functools
import math

import jax
import jax.numpy as jnp
import numpy as np
from jax import lax
from jax.experimental import pallas as pl
from jax.experimental.pallas import tpu as pltpu
from jax.sharding import PartitionSpec as P

NV = 10
NZ = 16
NY = 8
HALF = NV // 2
PER = HALF**3
LANES = 128

vel_bound = 4.0
courant = 0.08
time_step = 0.08
base_rate = 0.25
visc_index = 0.81
limiter_eps = 0.01
spacing = 2.0 * vel_bound / NV
quad = spacing**3 * (2.0 * math.pi) ** (-1.5)
unit = 0.5 * spacing
log2e = math.log2(math.e)

VMEM = pl.BlockSpec(memory_space=pltpu.VMEM)
SMEM = pl.BlockSpec(memory_space=pltpu.SMEM)
NT = (((1,), (1,)), ((), ()))
TN = (((0,), (0,)), ((), ()))
F32 = jnp.float32
BF16 = jnp.bfloat16


def tables():
    within = np.arange(PER)
    size = np.stack([within // HALF**2, within // HALF % HALF, within % HALF]) * 2 + 1
    feature = np.zeros((8, 8, LANES), np.float32)
    half = np.zeros((8, 8, LANES), np.float32)
    for octant in range(8):
        sign = np.array([1 - 2 * (octant >> 2 & 1), 1 - 2 * (octant >> 1 & 1), 1 - 2 * (octant & 1)])
        feature[octant, 0, :PER] = 1
        feature[octant, 1:4, :PER] = size * sign[:, None]
        feature[octant, 4, :PER] = (size * size).sum(0)
        half[octant, :3, :PER] = 0.5 * courant * unit * size
    pad = np.zeros_like(feature)
    phi = np.concatenate([feature, feature, feature, pad], axis=1)
    weight = np.concatenate([feature, pad], axis=1)
    keep = np.zeros((32, LANES), np.float32)
    keep[[5, 13, 21]] = 1
    return (
        jnp.asarray(phi, BF16),
        jnp.asarray(keep, BF16),
        jnp.asarray(weight, BF16),
        jnp.asarray(half, F32),
    )


def slope(left, right, left_sq, right_sq):
    return (left * right) * (left + right) * (1.0 / (left_sq + right_sq))


def place_octant(octant):
    pos_y = octant // 2 % 2 == 0
    pos_z = octant % 2 == 0
    roll_y = jnp.where(pos_y, 1, NY - 1)
    first = jnp.where(pos_z, 0, (NZ - 1) * NY)
    pace = jnp.where(pos_z, NY, -NY)
    offs = [pl.multiple_of(first + i * pace, NY) for i in range(NZ)]
    return roll_y, offs


def convert(load, store, tmp, octants):
    for o in range(octants):
        x = load(o)
        x = jnp.concatenate([x, jnp.zeros((LANES - PER, LANES), F32)], 0)
        tmp[o] = x.T
        for z in range(NZ):
            store(o, z, tmp[o, pl.ds(z, NY, stride=NZ), :])


def coefficients(total, scale):
    m0 = total[0:1]
    inv = 1.0 / m0
    ux = unit * total[1:2] * inv
    uy = unit * total[2:3] * inv
    uz = unit * total[3:4] * inv
    square = ux * ux + uy * uy + uz * uz
    temper = (unit * unit * total[4:5] * inv - square) * (1.0 / 3.0)
    log_t = jnp.log2(temper)
    density = quad * m0
    pace = (time_step * base_rate) * scale * density
    keep = 1.0 - pace * jnp.exp2((1.0 - visc_index) * log_t)
    beta = log2e / temper
    c0 = jnp.log2(pace * density) + (1.0 - visc_index - 1.5) * log_t - 0.5 * beta * square
    slow = unit * beta
    row = lax.broadcasted_iota(jnp.int32, (8, LANES), 0)
    c = jnp.where(row == 0, c0, 0.0)
    c = jnp.where(row == 1, slow * ux, c)
    c = jnp.where(row == 2, slow * uy, c)
    c = jnp.where(row == 3, slow * uz, c)
    c = jnp.where(row == 4, (-0.5 * unit) * slow, c)
    c = jnp.where(row == 5, keep, c)
    high = c.astype(BF16).astype(F32)
    rest = c - high
    middle = rest.astype(BF16).astype(F32)
    low = rest - middle
    return jnp.concatenate([high, middle, low, jnp.zeros_like(c)], 0).astype(BF16)


def moments_of(x, weight):
    high = x.astype(BF16)
    low = (x - high.astype(F32)).astype(BF16)
    m = lax.dot_general(weight, high, NT, preferred_element_type=F32)
    m = m + lax.dot_general(weight, low, NT, preferred_element_type=F32)
    return m[:8]


def prepare(js, coef, tabs, keep_ref):
    for n, j in enumerate(js):
        keep_ref[n] = lax.dot_general(coef[j], tabs[1][...], TN, preferred_element_type=F32)


def advance(js, get, o, octant, place, coef, tabs, arg, keep_ref, carry, emit):
    roll_y, offs = place
    back_y = NY - roll_y
    half = tabs[3][octant]
    hx, hy, hz = half[0:1], half[1:2], half[2:3]
    for n, j in enumerate(js):
        arg[n] = lax.dot_general(coef[j], tabs[0][octant], TN, preferred_element_type=F32)

    def rd(j, i):
        ref, index = get(j)
        return ref[index, o, pl.ds(offs[i % NZ], NY), :]

    eps2 = 0.5 * limiter_eps
    j = js[0] - 1
    for i in range(NZ):
        x = rd(j, i)
        a = x - rd(j - 1, i)
        b = rd(j + 1, i) - x
        bb = b * b + eps2
        s = pl.ds(i * NY, NY)
        carry[0, s, :] = (x + x) + slope(a, b, a * a + eps2, bb)
        carry[1, s, :] = b
        carry[2, s, :] = bb
    for n, j in enumerate(js):
        xm2, xm1, x0 = rd(j, NZ - 2), rd(j, NZ - 1), rd(j, 0)
        am, az = xm1 - xm2, x0 - xm1
        ez = az * az + eps2
        gz = (xm1 + xm1) + slope(am, az, am * am + eps2, ez)
        for i in range(NZ):
            s = pl.ds(i * NY, NY)
            x, xn = x0, rd(j, i + 1)
            x2 = x + x
            an = xn - x
            en = an * an + eps2
            gn = x2 + slope(az, an, ez, en)
            acc = hz * (gn - gz)
            az, ez, gz, x0 = an, en, gn, xn
            b = rd(j + 1, i) - x
            bb = b * b + eps2
            g = x2 + slope(carry[1, s, :], b, carry[2, s, :], bb)
            acc = acc + hx * (g - carry[0, s, :])
            carry[0, s, :] = g
            carry[1, s, :] = b
            carry[2, s, :] = bb
            a = x - pltpu.roll(x, roll_y, 0)
            b = pltpu.roll(a, back_y, 0)
            g = x2 + slope(a, b, a * a + eps2, b * b + eps2)
            acc = acc + hy * (g - pltpu.roll(g, roll_y, 0))
            z = pl.ds(offs[i], NY)
            emit(j, i, x * keep_ref[n, z, :] + (jnp.exp2(arg[n, z, :]) - acc))


def flip(neg, count, i):
    return jnp.where(neg, count - 1 - i, i)


def load_natural(ref, index):
    return lambda o: ref[index, o * PER : (o + 1) * PER, :]


def store_tile(ref, index):
    def store(o, z, value):
        ref[index, o, z * NY : (z + 1) * NY, :] = value

    return store


def start_kernel(info, x, *refs):
    tabs, (tiles, mom, tmp) = refs[:4], refs[4:]
    layers, octants = tiles.shape[0], tiles.shape[1]
    neg, first = info[0] != 0, info[1]
    for j in range(layers):
        nat = flip(neg, layers, j)
        convert(load_natural(x, nat), store_tile(tiles, j), tmp, octants)
        total = 0.0
        for o in range(octants):
            total = total + moments_of(tiles[j, o], tabs[2][first + o])
        mom[nat] = total


def share_kernel(info, ma, mb, scale, heavy, light):
    layers = ma.shape[0]
    neg = info[0] != 0
    row = lax.broadcasted_iota(jnp.int32, (8, LANES), 0)

    def packed(j):
        nat = flip(neg, layers, j)
        return jnp.where(row == 5, scale[nat], ma[nat] + mb[nat])

    for i in range(4):
        heavy[i] = packed(layers - 4 + i)
    for i in range(2):
        light[i] = packed(i)


def first_kernel(info, tiles, h1, l1, ma, mb, scale, *refs):
    tabs = refs[:4]
    new, side, mom, tmp, arg, keep, carry, coef = refs[4:]
    layers, octants = tiles.shape[0], tiles.shape[1]
    neg, first = info[0] != 0, info[1]
    for i in range(2):
        convert(load_natural(h1, flip(neg, 2, i)), store_tile(side, i), tmp, octants)
    convert(load_natural(l1, 0), store_tile(side, 2), tmp, octants)
    js = list(range(layers))
    for j in js:
        nat = flip(neg, layers, j)
        coef[j] = coefficients(ma[nat] + mb[nat], scale[nat])
        mom[nat] = jnp.zeros((8, LANES), F32)
    prepare(js, coef, tabs, keep)

    def get(j):
        return (side, j + 2) if j < 0 else (side, 2) if j == layers else (tiles, j)

    @pl.loop(0, octants)
    def _(o):
        place = place_octant(first + o)

        def emit(j, i, value):
            new[j, o, pl.ds(place[1][i], NY), :] = value

        advance(js, get, o, first + o, place, coef, tabs, arg, keep, carry, emit)
        for j in js:
            nat = flip(neg, layers, j)
            mom[nat] += moments_of(new[j, o], tabs[2][first + o])


def second_kernel(info, tiles, side, h2, l2, sh, sl, new, ma, mb, scale, *refs):
    tabs = refs[:4]
    edge, far, newer, mom, tmp, arg, keep, carry, coef, last = refs[4:]
    layers, octants = tiles.shape[0], tiles.shape[1]
    neg, first = info[0] != 0, info[1]
    for i in range(2):
        convert(load_natural(h2, flip(neg, 2, i)), store_tile(far, i), tmp, octants)
        convert(load_natural(l2, flip(neg, 2, i)), store_tile(last, i), tmp, octants)
    up, down, own = [-2, -1], [layers, layers + 1], list(range(layers))
    outer = {}
    for i in range(2):
        coef[i] = coefficients(sh[2 + i], sh[2 + i, 5:6])
        coef[2 + i] = coefficients(sl[i], sl[i, 5:6])
    for j in own:
        nat = flip(neg, layers, j)
        coef[4 + j] = coefficients(ma[nat] + mb[nat], scale[nat])
    outer = {-2: 0, -1: 1, layers: 2, layers + 1: 3}
    at_outer = {j: coef.at[n] for j, n in outer.items()}
    at_own = {j: coef.at[4 + j] for j in own}
    co = {j: r[...] for j, r in at_outer.items()}
    cn = {j: r[...] for j, r in at_own.items()}
    prepare(up + down, co, tabs, keep)
    prepare(own, cn, tabs, keep.at[4:])
    for n in range(mom.shape[0]):
        mom[n] = jnp.zeros((8, LANES), F32)

    def get0(j):
        if j < -2:
            return far, j + 4
        if j < 0:
            return side, j + 2
        if j > layers:
            return last, j - layers - 1
        return (side, 2) if j == layers else (tiles, j)

    def get1(j):
        return (edge, outer[j]) if j in outer else (new, j)

    @pl.loop(0, octants)
    def _(o):
        octant = first + o
        place = place_octant(octant)

        def emit1(j, i, value):
            edge[outer[j], o, pl.ds(place[1][i], NY), :] = value

        def emit2(j, i, value):
            newer[j, o, pl.ds(place[1][i], NY), :] = value

        advance(up, get0, o, octant, place, co, tabs, arg, keep, carry, emit1)
        advance(down, get0, o, octant, place, co, tabs, arg.at[2:], keep.at[2:], carry, emit1)
        advance(own, get1, o, octant, place, cn, tabs, arg.at[4:], keep.at[4:], carry, emit2)
        for j, n in outer.items():
            mom[2 + flip(neg, layers, j)] += moments_of(edge[n, o], tabs[2][octant])
        for j in own:
            nat = flip(neg, layers, j)
            mom[layers + 4 + nat] += moments_of(newer[j, o], tabs[2][octant])


def third_kernel(info, side, far, h3, sh, *refs):
    tabs = refs[:4]
    rim, tmp, arg, keep, carry, coef, last = refs[4:]
    octants = side.shape[1]
    neg, first = info[0] != 0, info[1]
    for i in range(2):
        convert(load_natural(h3, flip(neg, 2, i)), store_tile(last, i), tmp, octants)
    js = [-4, -3]
    co = {}
    for i, j in enumerate(js):
        co[j] = coefficients(sh[i], sh[i, 5:6])
    prepare(js, co, tabs, keep)

    def get(j):
        return (last, j + 6) if j < -4 else (far, j + 4) if j < -2 else (side, j + 2)

    @pl.loop(0, octants)
    def _(o):
        place = place_octant(first + o)

        def emit(j, i, value):
            rim[j + 4, o, pl.ds(place[1][i], NY), :] = value

        advance(js, get, o, first + o, place, co, tabs, arg, keep, carry, emit)


def last_kernel(info, rim, edge, new, newer, ma, mb, sh, sl, scale, *refs):
    tabs = refs[:4]
    out, tmp, arg, keep, carry, beside, result = refs[4:]
    layers, octants = new.shape[0], new.shape[1]
    neg, first = info[0] != 0, info[1]
    up, down, own = [-2, -1], [layers], list(range(layers))
    outer = {-2: 0, -1: 1, layers: 2, layers + 1: 3}
    co, cn = {}, {}
    for j in up + down:
        slot = 2 + flip(neg, layers, j)
        pace = sl[0, 5:6] if j == layers else sh[4 + j, 5:6]
        co[j] = coefficients(ma[slot] + mb[slot], pace)
    for j in own:
        nat = flip(neg, layers, j)
        cn[j] = coefficients(ma[layers + 4 + nat] + mb[layers + 4 + nat], scale[nat])
    prepare(up + down, co, tabs, keep)
    prepare(own, cn, tabs, keep.at[3:])

    def get1(j):
        return (rim, j + 4) if j < -2 else (edge, outer[j]) if j in outer else (new, j)

    def get2(j):
        return (beside, outer[j]) if j in outer else (newer, j)

    @pl.loop(0, octants)
    def _(o):
        octant = first + o
        place = place_octant(octant)
        starts = [place[1][i] // NY for i in range(NZ)]

        def emit2(j, i, value):
            beside[outer[j], o, pl.ds(place[1][i], NY), :] = value

        def emit3(j, i, value):
            result[j, o, pl.ds(starts[i], NY, stride=NZ), :] = value

        advance(up, get1, o, octant, place, co, tabs, arg, keep, carry, emit2)
        advance(down, get1, o, octant, place, co, tabs, arg.at[2:], keep.at[2:], carry, emit2)
        advance(own, get2, o, octant, place, cn, tabs, arg.at[3:], keep.at[3:], carry, emit3)

    for j in own:
        nat = flip(neg, layers, j)
        for o in range(octants):
            out[nat, o * PER : (o + 1) * PER, :] = result[j, o].T[:PER]


def scratch(octants, layers, extra=()):
    square = (LANES, LANES)
    return [
        pltpu.VMEM((octants, *square), F32),
        pltpu.VMEM((layers, *square), F32),
        pltpu.VMEM((layers, *square), F32),
        pltpu.VMEM((3, *square), F32),
        *extra,
    ]


def run(body, name, args, outs, scratch_shapes):
    return pl.pallas_call(
        body,
        name=name,
        out_shape=[jax.ShapeDtypeStruct(shape, F32) for shape in outs],
        in_specs=[SMEM] + [VMEM] * (len(args) - 1),
        out_specs=[VMEM] * len(outs),
        scratch_shapes=scratch_shapes,
        compiler_params=pltpu.CompilerParams(vmem_limit_bytes=24 * 2**20),
    )(*args)


def exchange(part, axis):
    count = lax.axis_size(axis)
    if count == 1:
        return part, jnp.zeros_like(part)
    if count & (count - 1):
        return lax.psum(part, axis), jnp.zeros_like(part)
    bit = 1
    while True:
        other = lax.ppermute(part, axis, [(i, i ^ bit) for i in range(count)])
        bit *= 2
        if bit == count:
            return part, other
        part = part + other


def per_device(distribution, collision_scale):
    vel_count, layers, _ = distribution.shape
    oct_count, ring = lax.axis_size("oct"), lax.axis_size("space")
    octants = vel_count // PER
    assert vel_count % PER == 0 and oct_count % 2 == 0 and layers >= 6
    first = lax.axis_index("oct") * octants
    neg = first // 4 % 2
    info = jnp.stack([neg, first]).astype(jnp.int32)
    toward = []
    for o in range(oct_count):
        step = -1 if o * octants // 4 % 2 else 1
        for s in range(ring):
            toward.append((o * ring + s, o * ring + (s + step) % ring))
    against = [(target, source) for source, target in toward]

    def send(block, pairs):
        return lax.ppermute(block, ("oct", "space"), pairs)

    def cut(low, high, count):
        start = jnp.where(neg == 1, low, high)
        return lax.dynamic_slice_in_dim(x, start, count, 0)

    x = jnp.transpose(distribution, (1, 0, 2))
    h1 = send(cut(0, layers - 2, 2), toward)
    l1 = send(cut(layers - 1, 0, 1), against)
    h2 = send(cut(2, layers - 4, 2), toward)
    l2 = send(cut(layers - 3, 1, 2), against)
    scale = collision_scale.reshape(layers, NY, NZ).transpose(0, 2, 1).reshape(layers, 1, LANES)
    tabs = tables()
    tile = (octants, LANES, LANES)
    coef = pltpu.VMEM((layers + 4, 32, LANES), BF16)
    tiles, m0 = run(
        start_kernel,
        "start",
        (info, x, *tabs),
        [(layers, *tile), (layers, 8, LANES)],
        [pltpu.VMEM(tile, F32)],
    )
    m0 = exchange(m0, "oct")
    sh, sl = run(
        share_kernel, "share", (info, *m0, scale), [(4, 8, LANES), (2, 8, LANES)], []
    )
    sh, sl = send(sh, toward), send(sl, against)
    h3 = send(cut(4, layers - 6, 2), toward)
    new, side, m1 = run(
        first_kernel,
        "first",
        (info, tiles, h1, l1, *m0, scale, *tabs),
        [(layers, *tile), (3, *tile), (layers, 8, LANES)],
        scratch(octants, layers, [coef]),
    )
    m1 = exchange(m1, "oct")
    edge, far, newer, m2 = run(
        second_kernel,
        "second",
        (info, tiles, side, h2, l2, sh, sl, new, *m1, scale, *tabs),
        [(4, *tile), (2, *tile), (layers, *tile), (2 * layers + 4, 8, LANES)],
        scratch(octants, layers + 4, [coef, pltpu.VMEM((2, *tile), F32)]),
    )
    m2 = exchange(m2, "oct")
    (rim,) = run(
        third_kernel,
        "third",
        (info, side, far, h3, sh, *tabs),
        [(2, *tile)],
        scratch(octants, 2, [coef, pltpu.VMEM((2, *tile), F32)]),
    )
    (out,) = run(
        last_kernel,
        "last",
        (info, rim, edge, new, newer, *m2, sh, sl, scale, *tabs),
        [(layers, vel_count, LANES)],
        scratch(
            octants, layers + 3, [pltpu.VMEM((3, *tile), F32), pltpu.VMEM((layers, *tile), F32)]
        ),
    )
    return jnp.transpose(out, (1, 0, 2))


def solution(mesh):
    return jax.shard_map(
        per_device,
        mesh=mesh,
        in_specs=(P("oct", "space", None), P(None, "space", None)),
        out_specs=P("oct", "space", None),
        check_vma=False,
    )
```

```python
import math

import jax
import jax.numpy as jnp
import numpy as np
from jax import lax
from jax.experimental import pallas as pl
from jax.experimental.pallas import tpu as pltpu
from jax.sharding import PartitionSpec as P


NV = 10
NZ = 16
NY = 8
HALF = NV // 2
PER = HALF**3
LANES = 128

vel_bound = 4.0
courant = 0.08
time_step = 0.08
base_rate = 0.25
visc_index = 0.81
limiter_eps = 0.01
spacing = 2.0 * vel_bound / NV
quad = spacing**3 * (2.0 * math.pi) ** (-1.5)
unit = 0.5 * spacing
log2e = math.log2(math.e)

VMEM = pl.BlockSpec(memory_space=pltpu.VMEM)
HBM = pl.BlockSpec(memory_space=pltpu.HBM)
SMEM = pl.BlockSpec(memory_space=pltpu.SMEM)
NT = (((1,), (1,)), ((), ()))
TN = (((0,), (0,)), ((), ()))
F32 = jnp.float32
BF16 = jnp.bfloat16


def table():
    within = np.arange(PER)
    size = np.stack([within // HALF**2, within // HALF % HALF, within % HALF]) * 2 + 1
    feature = np.zeros((9, 8, LANES), np.float32)
    for octant in range(8):
        sign = np.array([1 - 2 * (octant >> 2 & 1), 1 - 2 * (octant >> 1 & 1), 1 - 2 * (octant & 1)])
        feature[octant, 0, :PER] = 1
        feature[octant, 1:4, :PER] = size * sign[:, None]
        feature[octant, 4, :PER] = (size * size).sum(0)
    feature[8, 5] = 1
    pad = np.zeros_like(feature)
    return jnp.asarray(np.concatenate([feature, feature, feature, pad, feature, pad], axis=1), BF16)


def phi(tab, octant):
    return tab[octant, 0:32]


def weight(tab, octant):
    return tab[octant, 32:48]


def slope(left, right, left_sq, right_sq):
    return (left * right) * (left + right) * (1.0 / (left_sq + right_sq))


def place_octant(octant):
    pos_y = octant // 2 % 2 == 0
    pos_z = octant % 2 == 0
    roll_y = jnp.where(pos_y, 1, NY - 1)
    first = jnp.where(pos_z, 0, (NZ - 1) * NY)
    pace = jnp.where(pos_z, NY, -NY)
    offs = [pl.multiple_of(first + i * pace, NY) for i in range(NZ)]
    return roll_y, offs


def convert(load, store, tmp, octants):
    for o in range(octants):
        x = load(o)
        x = jnp.concatenate([x, jnp.zeros((LANES - PER, LANES), F32)], 0)
        tmp[o] = x.T
        for z in range(NZ):
            store(o, z, tmp[o, pl.ds(z, NY, stride=NZ), :])


def coefficients(total, scale):
    m0 = total[0:1]
    inv = 1.0 / m0
    ux = unit * total[1:2] * inv
    uy = unit * total[2:3] * inv
    uz = unit * total[3:4] * inv
    square = ux * ux + uy * uy + uz * uz
    temper = (unit * unit * total[4:5] * inv - square) * (1.0 / 3.0)
    log_t = jnp.log2(temper)
    density = quad * m0
    pace = (time_step * base_rate) * scale * density
    keep = 1.0 - pace * jnp.exp2((1.0 - visc_index) * log_t)
    beta = log2e / temper
    c0 = jnp.log2(pace * density) + (1.0 - visc_index - 1.5) * log_t - 0.5 * beta * square
    slow = unit * beta
    row = lax.broadcasted_iota(jnp.int32, (8, LANES), 0)
    c = jnp.where(row == 0, c0, 0.0)
    c = jnp.where(row == 1, slow * ux, c)
    c = jnp.where(row == 2, slow * uy, c)
    c = jnp.where(row == 3, slow * uz, c)
    c = jnp.where(row == 4, (-0.5 * unit) * slow, c)
    c = jnp.where(row == 5, keep, c)
    high = c.astype(BF16).astype(F32)
    rest = c - high
    middle = rest.astype(BF16).astype(F32)
    low = rest - middle
    return jnp.concatenate([high, middle, low, jnp.zeros_like(c)], 0).astype(BF16)


def moments_of(x, rows):
    high = x.astype(BF16)
    low = (x - high.astype(F32)).astype(BF16)
    m = lax.dot_general(rows, high, NT, preferred_element_type=F32)
    m = m + lax.dot_general(rows, low, NT, preferred_element_type=F32)
    return m[:8]


def prepare(js, coef, tab, keep_ref):
    for n, j in enumerate(js):
        keep_ref[n] = lax.dot_general(coef[j], phi(tab, 8), TN, preferred_element_type=F32)


def advance(js, get, o, octant, place, coef, tab, arg, keep_ref, carry, emit):
    roll_y, offs = place
    back_y = NY - roll_y
    half = (0.5 * courant * unit) * jnp.abs(weight(tab, octant).astype(F32))
    hx, hy, hz = half[1:2], half[2:3], half[3:4]
    for n, j in enumerate(js):
        arg[n] = lax.dot_general(coef[j], phi(tab, octant), TN, preferred_element_type=F32)

    def rd(j, i):
        ref, index = get(j)
        return ref[index, o, pl.ds(offs[i % NZ], NY), :]

    def square(d, index):
        return d * d + limiter_eps if index % 2 == 0 else d * d

    j = js[0] - 1
    for i in range(NZ):
        x = rd(j, i)
        a = x - rd(j - 1, i)
        b = rd(j + 1, i) - x
        bb = square(b, j)
        s = pl.ds(i * NY, NY)
        carry[0, s, :] = (x + x) + slope(a, b, square(a, j - 1), bb)
        carry[1, s, :] = b
        carry[2, s, :] = bb
    for n, j in enumerate(js):
        xm2, xm1, x0 = rd(j, NZ - 2), rd(j, NZ - 1), rd(j, 0)
        am, az = xm1 - xm2, x0 - xm1
        ez = square(az, NZ - 1)
        gz = (xm1 + xm1) + slope(am, az, square(am, NZ - 2), ez)
        for i in range(NZ):
            s = pl.ds(i * NY, NY)
            x, xn = x0, rd(j, i + 1)
            x2 = x + x
            an = xn - x
            en = square(an, i)
            gn = x2 + slope(az, an, ez, en)
            acc = hz * (gn - gz)
            az, ez, gz, x0 = an, en, gn, xn
            b = rd(j + 1, i) - x
            bb = square(b, j)
            g = x2 + slope(carry[1, s, :], b, carry[2, s, :], bb)
            acc = acc + hx * (g - carry[0, s, :])
            carry[0, s, :] = g
            carry[1, s, :] = b
            carry[2, s, :] = bb
            a = x - pltpu.roll(x, roll_y, 0)
            aa = a * a + 0.5 * limiter_eps
            g = x2 + slope(a, pltpu.roll(a, back_y, 0), aa, pltpu.roll(aa, back_y, 0))
            acc = acc + hy * (g - pltpu.roll(g, roll_y, 0))
            z = pl.ds(offs[i], NY)
            emit(j, i, x * keep_ref[n, z, :] + (jnp.exp2(arg[n, z, :]) - acc))


def flip(neg, count, i):
    return jnp.where(neg, count - 1 - i, i)


def load_natural(ref, index):
    return lambda o: ref[index, o * PER : (o + 1) * PER, :]


def store_tile(ref, index):
    def store(o, z, value):
        ref[index, o, z * NY : (z + 1) * NY, :] = value

    return store


def cut_kernel(info, x, h1, l1, copy, sems, out_sems):
    layers = copy.shape[0]
    neg = info[0] != 0
    base = jnp.where(neg, 0, layers - 2)
    order = [layers - 2, layers - 1, 0, *range(1, layers - 2)]
    places = [flip(neg, layers, j) for j in order]
    loads = [pltpu.make_async_copy(x.at[n], copy.at[n], sems.at[i]) for i, n in enumerate(places)]
    targets = [h1.at[places[0] - base], h1.at[places[1] - base], l1.at[0]]
    stores = [
        pltpu.make_async_copy(copy.at[places[i]], target, out_sems.at[i])
        for i, target in enumerate(targets)
    ]
    for load in loads:
        load.start()
    for load, store in zip(loads, stores):
        load.wait()
        store.start()
    for load in loads[3:]:
        load.wait()
    for store in stores:
        store.wait()


def start_kernel(info, x, raw, tab, tiles, mom, scale, h2, h3, l2, tmp, sems):
    layers, octants = tiles.shape[0], tiles.shape[1]
    neg, first = info[0] != 0, info[1]
    starts = [jnp.where(neg, 2, layers - 4), jnp.where(neg, 4, layers - 6), jnp.where(neg, layers - 3, 1)]
    copies = [
        pltpu.make_async_copy(x.at[pl.ds(begin, 2)], target, sems.at[i])
        for i, (begin, target) in enumerate(zip(starts, (h2, h3, l2)))
    ]
    for c in copies:
        c.start()
    for j in range(layers):
        nat = flip(neg, layers, j)
        convert(load_natural(x, nat), store_tile(tiles, j), tmp, octants)
        total = 0.0
        for o in range(octants):
            total = total + moments_of(tiles[j, o], weight(tab, first + o))
        mom[nat] = total
    padded = jnp.concatenate([raw[0], jnp.zeros((LANES - layers, LANES), F32)], 0)
    tmp[0] = padded.T
    mixed = jnp.concatenate([tmp[0, pl.ds(z, NY, stride=NZ), :] for z in range(NZ)], 0).T
    for n in range(layers):
        scale[n] = mixed[n : n + 1]
    for c in copies:
        c.wait()


def share_kernel(ma, mb, scale, out):
    row = lax.broadcasted_iota(jnp.int32, (8, LANES), 0)
    for n in range(ma.shape[0]):
        out[n] = jnp.where(row == 5, scale[n], ma[n] + mb[n])


def first_kernel(info, tiles, h1, l1, ma, mb, scale, *refs):
    tab = refs[0]
    new, side, mom, tmp, arg, keep, carry = refs[1:]
    layers, octants = tiles.shape[0], tiles.shape[1]
    neg, first = info[0] != 0, info[1]
    for i in range(2):
        convert(load_natural(h1, flip(neg, 2, i)), store_tile(side, i), tmp, octants)
    convert(load_natural(l1, 0), store_tile(side, 2), tmp, octants)
    js = list(range(layers))
    co = {}
    for j in js:
        nat = flip(neg, layers, j)
        co[j] = coefficients(ma[nat] + mb[nat], scale[nat])
        mom[nat] = jnp.zeros((8, LANES), F32)
    prepare(js, co, tab, keep)
    outer = {-2: 0, -1: 1, layers: 2}

    def get(j):
        return (side, outer[j]) if j in outer else (tiles, j)

    @pl.loop(0, octants)
    def _(o):
        octant = first + o
        place = place_octant(octant)

        def emit(j, i, value):
            new[j, o, pl.ds(place[1][i], NY), :] = value

        advance(js, get, o, octant, place, co, tab, arg, keep, carry, emit)
        for j in js:
            mom[flip(neg, layers, j)] += moments_of(new[j, o], weight(tab, octant))


def edge_kernel(info, tiles, side, h2, l2, up_share, down_share, *refs):
    tab = refs[0]
    edge, far, mom, tmp, arg, keep, carry, below = refs[1:]
    layers, octants = tiles.shape[0], tiles.shape[1]
    neg, first = info[0] != 0, info[1]
    for i in range(2):
        convert(load_natural(h2, flip(neg, 2, i)), store_tile(far, i), tmp, octants)
        convert(load_natural(l2, flip(neg, 2, i)), store_tile(below, i), tmp, octants)
    up, down = [-2, -1], [layers, layers + 1]
    outer = {-2: 0, -1: 1, layers: 2, layers + 1: 3}
    co = {}
    for j in outer:
        if j < 0:
            known = up_share[flip(neg, layers, layers + j)]
        else:
            known = down_share[flip(neg, layers, j - layers)]
        co[j] = coefficients(known, known[5:6])
    prepare(up + down, co, tab, keep)
    for n in range(4):
        mom[n] = jnp.zeros((8, LANES), F32)

    def get(j):
        if j < -2:
            return far, j + 4
        if j < 0:
            return side, j + 2
        if j > layers:
            return below, j - layers - 1
        return (side, 2) if j == layers else (tiles, j)

    @pl.loop(0, octants)
    def _(o):
        octant = first + o
        place = place_octant(octant)

        def emit(j, i, value):
            edge[outer[j], o, pl.ds(place[1][i], NY), :] = value

        advance(up, get, o, octant, place, co, tab, arg, keep, carry, emit)
        advance(down, get, o, octant, place, co, tab, arg.at[2:], keep.at[2:], carry, emit)
        for n in range(4):
            mom[flip(neg, 4, n)] += moments_of(edge[n, o], weight(tab, octant))


def middle_kernel(info, new, ma, mb, scale, *refs):
    tab = refs[0]
    newer, mom, _, arg, keep, carry = refs[1:]
    layers, octants = new.shape[0], new.shape[1]
    neg, first = info[0] != 0, info[1]
    js = list(range(2, layers - 1))
    co = {}
    for j in js:
        nat = flip(neg, layers, j)
        co[j] = coefficients(ma[nat] + mb[nat], scale[nat])
        mom[j - 2] = jnp.zeros((8, LANES), F32)
    prepare(js, co, tab, keep)

    @pl.loop(0, octants)
    def _(o):
        octant = first + o
        place = place_octant(octant)

        def emit(j, i, value):
            newer[j - 2, o, pl.ds(place[1][i], NY), :] = value

        advance(js, lambda j: (new, j), o, octant, place, co, tab, arg, keep, carry, emit)
        for j in js:
            mom[j - 2] += moments_of(newer[j - 2, o], weight(tab, octant))


def second_kernel(info, new, edge, ma, mb, middle, scale, *refs):
    tab = refs[0]
    newer, mom, _, arg, keep, carry = refs[1:]
    layers, octants = new.shape[0], new.shape[1]
    neg, first = info[0] != 0, info[1]
    up, down = [0, 1], [layers - 1]
    slots = {0: 0, 1: 1, layers - 1: 2}
    co = {}
    for j in slots:
        nat = flip(neg, layers, j)
        co[j] = coefficients(ma[nat] + mb[nat], scale[nat])
        mom[nat] = jnp.zeros((8, LANES), F32)
    for j in range(2, layers - 1):
        mom[flip(neg, layers, j)] = middle[j - 2]
    prepare(up + down, co, tab, keep)
    outer = {-2: 0, -1: 1, layers: 2}

    def get(j):
        return (edge, outer[j]) if j in outer else (new, j)

    @pl.loop(0, octants)
    def _(o):
        octant = first + o
        place = place_octant(octant)

        def emit(j, i, value):
            newer[slots[j], o, pl.ds(place[1][i], NY), :] = value

        advance(up, get, o, octant, place, co, tab, arg, keep, carry, emit)
        advance(down, get, o, octant, place, co, tab, arg.at[2:], keep.at[2:], carry, emit)
        for j, n in slots.items():
            mom[flip(neg, layers, j)] += moments_of(newer[n, o], weight(tab, octant))


def third_kernel(info, side, far, h3, edge, new, ma, mb, up_share, down_share, *refs):
    tab = refs[0]
    beside, tmp, arg, keep, carry, last, rim = refs[1:]
    layers, octants = new.shape[0], new.shape[1]
    neg, first = info[0] != 0, info[1]
    for i in range(2):
        convert(load_natural(h3, flip(neg, 2, i)), store_tile(last, i), tmp, octants)
    js, up, down = [-4, -3], [-2, -1], [layers]
    outer = {-2: 0, -1: 1, layers: 2, layers + 1: 3}
    co = {}
    for j in js:
        known = up_share[flip(neg, layers, layers + j)]
        co[j] = coefficients(known, known[5:6])
    for i, j in enumerate(up + down):
        slot = flip(neg, 4, i)
        beyond = up_share[flip(neg, layers, layers + j)] if j < 0 else down_share[flip(neg, layers, 0)]
        co[j] = coefficients(ma[slot] + mb[slot], beyond[5:6])
    prepare(js + up + down, co, tab, keep)

    def get0(j):
        return (last, j + 6) if j < -4 else (far, j + 4) if j < -2 else (side, j + 2)

    def get1(j):
        return (rim, j + 4) if j < -2 else (edge, outer[j]) if j in outer else (new, j)

    @pl.loop(0, octants)
    def _(o):
        octant = first + o
        place = place_octant(octant)

        def emit1(j, i, value):
            rim[j + 4, o, pl.ds(place[1][i], NY), :] = value

        def emit2(j, i, value):
            beside[outer[j], o, pl.ds(place[1][i], NY), :] = value

        advance(down, get1, o, octant, place, co, tab, arg.at[4:], keep.at[4:], carry, emit2)
        advance(js, get0, o, octant, place, co, tab, arg, keep, carry, emit1)
        advance(up, get1, o, octant, place, co, tab, arg.at[2:], keep.at[2:], carry, emit2)


def last_kernel(info, middle, newer, beside, ma, mb, scale, *refs):
    tab = refs[0]
    out, _, arg, keep, carry, result = refs[1:]
    layers, octants = out.shape[0], newer.shape[1]
    neg, first = info[0] != 0, info[1]
    js = list(range(layers))
    outer = {-2: 0, -1: 1, layers: 2}
    slots = {0: 0, 1: 1, layers - 1: 2}
    co = {}
    for j in js:
        nat = flip(neg, layers, j)
        co[j] = coefficients(ma[nat] + mb[nat], scale[nat])
    prepare(js, co, tab, keep)

    def get(j):
        if j in outer:
            return beside, outer[j]
        return (newer, slots[j]) if j in slots else (middle, j - 2)

    @pl.loop(0, octants)
    def _(o):
        octant = first + o
        place = place_octant(octant)
        starts = [place[1][i] // NY for i in range(NZ)]

        def emit(j, i, value):
            result[j, o, pl.ds(starts[i], NY, stride=NZ), :] = value

        advance(js, get, o, octant, place, co, tab, arg, keep, carry, emit)

    for j in js:
        nat = flip(neg, layers, j)
        for o in range(octants):
            out[nat, o * PER : (o + 1) * PER, :] = result[j, o].T[:PER]


def scratch(octants, layers, extra=()):
    square = (LANES, LANES)
    return [
        pltpu.VMEM((octants, *square), F32),
        pltpu.VMEM((layers, *square), F32),
        pltpu.VMEM((layers, *square), F32),
        pltpu.VMEM((3, *square), F32),
        *extra,
    ]


def run(body, args, outs, scratch_shapes, far_args=(), far_outs=()):
    call = pl.pallas_call(
        body,
        out_shape=[
            pltpu.HBM(shape, F32) if i in far_outs else jax.ShapeDtypeStruct(shape, F32)
            for i, shape in enumerate(outs)
        ],
        in_specs=[
            SMEM if a.dtype == jnp.int32 else HBM if i in far_args else VMEM for i, a in enumerate(args)
        ],
        out_specs=[HBM if i in far_outs else VMEM for i in range(len(outs))],
        scratch_shapes=scratch_shapes,
        compiler_params=pltpu.CompilerParams(vmem_limit_bytes=24 * 2**20),
    )
    args = [
        pltpu.with_memory_space_constraint(a, pltpu.HBM) if i in far_args else a
        for i, a in enumerate(args)
    ]
    return call(*args)


def exchange(part, axis):
    count = lax.axis_size(axis)
    if count == 1:
        return part, jnp.zeros_like(part)
    if count & (count - 1):
        return lax.psum(part, axis), jnp.zeros_like(part)
    bit = 1
    while True:
        other = lax.ppermute(part, axis, [(i, i ^ bit) for i in range(count)])
        bit *= 2
        if bit == count:
            return part, other
        part = part + other


def body(distribution, collision_scale):
    vel_count, layers, _ = distribution.shape
    oct_count, ring = lax.axis_size("oct"), lax.axis_size("space")
    octants = vel_count // PER
    assert vel_count % PER == 0 and oct_count % 2 == 0 and layers >= 6
    first = lax.axis_index("oct") * octants
    neg = first // 4 % 2
    info = jnp.stack([neg, first]).astype(jnp.int32)
    toward = []
    for o in range(oct_count):
        step = -1 if o * octants // 4 % 2 else 1
        for s in range(ring):
            toward.append((o * ring + s, o * ring + (s + step) % ring))
    against = [(target, source) for source, target in toward]

    def send(block, pairs):
        return lax.ppermute(block, ("oct", "space"), pairs)

    x = jnp.transpose(distribution, (1, 0, 2))
    tab = table()
    tile = (octants, LANES, LANES)
    rows = (8, LANES)
    block = (2, vel_count, LANES)
    two, six = pltpu.VMEM((2, *tile), F32), pltpu.VMEM((layers, *tile), F32)
    dma = pltpu.SemaphoreType.DMA
    h1, l1, x = run(
        cut_kernel,
        (info, x),
        [block, (1, vel_count, LANES), (layers, vel_count, LANES)],
        [dma((layers,)), dma((3,))],
        far_args=(1,),
        far_outs=(0, 1),
    )
    h1, l1 = send(h1, toward), send(l1, against)
    tiles, m0, scale, h2, h3, l2 = run(
        start_kernel,
        (info, x, collision_scale, tab),
        [(layers, *tile), (layers, *rows), (layers, 1, LANES), block, block, block],
        [pltpu.VMEM(tile, F32), dma((3,))],
        far_outs=(3, 4, 5),
    )
    m0 = exchange(m0, "oct")
    h2, h3, l2 = send(h2, toward), send(h3, toward), send(l2, against)
    (share,) = run(share_kernel, (*m0, scale), [(layers, *rows)], [])
    ch, cl = send(share, toward), send(share, against)
    new, side, m1 = run(
        first_kernel,
        (info, tiles, h1, l1, *m0, scale, tab),
        [(layers, *tile), (3, *tile), (layers, *rows)],
        scratch(octants, layers),
    )
    m1 = exchange(m1, "oct")
    edge, far, medge = run(
        edge_kernel,
        (info, tiles, side, h2, l2, ch, cl, tab),
        [(4, *tile), (2, *tile), (4, *rows)],
        scratch(octants, 4, [two]),
    )
    medge = exchange(medge, "oct")
    middle, mm = run(
        middle_kernel,
        (info, new, *m1, scale, tab),
        [(layers - 3, *tile), (layers - 3, *rows)],
        scratch(octants, layers - 3),
    )
    newer, m2 = run(
        second_kernel,
        (info, new, edge, *m1, mm, scale, tab),
        [(3, *tile), (layers, *rows)],
        scratch(octants, 3),
    )
    m2 = exchange(m2, "oct")
    (beside,) = run(
        third_kernel,
        (info, side, far, h3, edge, new, *medge, ch, cl, tab),
        [(3, *tile)],
        scratch(octants, 5, [two, two]),
    )
    (out,) = run(
        last_kernel,
        (info, middle, newer, beside, *m2, scale, tab),
        [(layers, vel_count, LANES)],
        scratch(octants, layers, [six]),
    )
    return jnp.transpose(out, (1, 0, 2))


def solution(mesh):
    return jax.shard_map(
        body,
        mesh=mesh,
        in_specs=(P("oct", "space", None), P(None, "space", None)),
        out_specs=P("oct", "space", None),
        check_vma=False,
    )
```

```python
import math

import jax
import jax.numpy as jnp
import numpy as np
from jax import lax
from jax.experimental import pallas as pl
from jax.experimental.pallas import tpu as pltpu
from jax.sharding import PartitionSpec as P


NV = 10
NZ = 16
NY = 8
HALF = NV // 2
PER = HALF**3
LANES = 128

vel_bound = 4.0
courant = 0.08
time_step = 0.08
base_rate = 0.25
visc_index = 0.81
limiter_eps = 0.01
spacing = 2.0 * vel_bound / NV
quad = spacing**3 * (2.0 * math.pi) ** (-1.5)
unit = 0.5 * spacing
log2e = math.log2(math.e)

VMEM = pl.BlockSpec(memory_space=pltpu.VMEM)
HBM = pl.BlockSpec(memory_space=pltpu.HBM)
SMEM = pl.BlockSpec(memory_space=pltpu.SMEM)
NT = (((1,), (1,)), ((), ()))
TN = (((0,), (0,)), ((), ()))
F32 = jnp.float32
BF16 = jnp.bfloat16


def table():
    within = np.arange(PER)
    size = np.stack([within // HALF**2, within // HALF % HALF, within % HALF]) * 2 + 1
    feature = np.zeros((9, 8, LANES), np.float32)
    for octant in range(8):
        sign = np.array([1 - 2 * (octant >> 2 & 1), 1 - 2 * (octant >> 1 & 1), 1 - 2 * (octant & 1)])
        feature[octant, 0, :PER] = 1
        feature[octant, 1:4, :PER] = size * sign[:, None]
        feature[octant, 4, :PER] = (size * size).sum(0)
    feature[8, 5] = 1
    pad = np.zeros_like(feature)
    return jnp.asarray(np.concatenate([feature, feature, feature, pad, feature, pad], axis=1), BF16)


def phi(tab, octant):
    return tab[octant, 0:32]


def weight(tab, octant):
    return tab[octant, 32:48]


def slope(left, right, left_sq, right_sq):
    return (left * right) * (left + right) * (1.0 / (left_sq + right_sq))


def place_octant(octant):
    pos_y = octant // 2 % 2 == 0
    pos_z = octant % 2 == 0
    roll_y = jnp.where(pos_y, 1, NY - 1)
    first = jnp.where(pos_z, 0, (NZ - 1) * NY)
    pace = jnp.where(pos_z, NY, -NY)
    offs = [pl.multiple_of(first + i * pace, NY) for i in range(NZ)]
    return roll_y, offs


def convert(load, store, tmp, octants):
    for o in range(octants):
        x = load(o)
        x = jnp.concatenate([x, jnp.zeros((LANES - PER, LANES), F32)], 0)
        tmp[o] = x.T
        for z in range(NZ):
            store(o, z, tmp[o, pl.ds(z, NY, stride=NZ), :])


def coefficients(total, scale):
    m0 = total[0:1]
    inv = 1.0 / m0
    ux = unit * total[1:2] * inv
    uy = unit * total[2:3] * inv
    uz = unit * total[3:4] * inv
    square = ux * ux + uy * uy + uz * uz
    temper = (unit * unit * total[4:5] * inv - square) * (1.0 / 3.0)
    log_t = jnp.log2(temper)
    density = quad * m0
    pace = (time_step * base_rate) * scale * density
    keep = 1.0 - pace * jnp.exp2((1.0 - visc_index) * log_t)
    beta = log2e / temper
    c0 = jnp.log2(pace * density) + (1.0 - visc_index - 1.5) * log_t - 0.5 * beta * square
    slow = unit * beta
    row = lax.broadcasted_iota(jnp.int32, (8, LANES), 0)
    c = jnp.where(row == 0, c0, 0.0)
    c = jnp.where(row == 1, slow * ux, c)
    c = jnp.where(row == 2, slow * uy, c)
    c = jnp.where(row == 3, slow * uz, c)
    c = jnp.where(row == 4, (-0.5 * unit) * slow, c)
    c = jnp.where(row == 5, keep, c)
    high = c.astype(BF16).astype(F32)
    rest = c - high
    middle = rest.astype(BF16).astype(F32)
    low = rest - middle
    return jnp.concatenate([high, middle, low, jnp.zeros_like(c)], 0).astype(BF16)


def moments_of(x, rows):
    high = x.astype(BF16)
    low = (x - high.astype(F32)).astype(BF16)
    m = lax.dot_general(rows, high, NT, preferred_element_type=F32)
    m = m + lax.dot_general(rows, low, NT, preferred_element_type=F32)
    return m[:8]


def prepare(js, coef, tab, keep_ref):
    for n, j in enumerate(js):
        keep_ref[n] = lax.dot_general(coef[j], phi(tab, 8), TN, preferred_element_type=F32)


def advance(js, get, o, octant, place, coef, tab, arg, keep_ref, carry, emit):
    roll_y, offs = place
    back_y = NY - roll_y
    half = (0.5 * courant * unit) * jnp.abs(weight(tab, octant).astype(F32))
    hx, hy, hz = half[1:2], half[2:3], half[3:4]
    for n, j in enumerate(js):
        arg[n] = lax.dot_general(coef[j], phi(tab, octant), TN, preferred_element_type=F32)

    def rd(j, i):
        ref, index = get(j)
        return ref[index, o, pl.ds(offs[i % NZ], NY), :]

    def square(d, index):
        return d * d + limiter_eps if index % 2 == 0 else d * d

    j = js[0] - 1
    for i in range(NZ):
        x = rd(j, i)
        a = x - rd(j - 1, i)
        b = rd(j + 1, i) - x
        bb = square(b, j)
        s = pl.ds(i * NY, NY)
        carry[0, s, :] = (x + x) + slope(a, b, square(a, j - 1), bb)
        carry[1, s, :] = b
        carry[2, s, :] = bb
    for n, j in enumerate(js):
        xm2, xm1, x0 = rd(j, NZ - 2), rd(j, NZ - 1), rd(j, 0)
        am, az = xm1 - xm2, x0 - xm1
        ez = square(az, NZ - 1)
        gz = (xm1 + xm1) + slope(am, az, square(am, NZ - 2), ez)
        for i in range(NZ):
            s = pl.ds(i * NY, NY)
            x, xn = x0, rd(j, i + 1)
            x2 = x + x
            an = xn - x
            en = square(an, i)
            gn = x2 + slope(az, an, ez, en)
            acc = hz * (gn - gz)
            az, ez, gz, x0 = an, en, gn, xn
            b = rd(j + 1, i) - x
            bb = square(b, j)
            g = x2 + slope(carry[1, s, :], b, carry[2, s, :], bb)
            acc = acc + hx * (g - carry[0, s, :])
            carry[0, s, :] = g
            carry[1, s, :] = b
            carry[2, s, :] = bb
            a = x - pltpu.roll(x, roll_y, 0)
            aa = a * a + 0.5 * limiter_eps
            g = x2 + slope(a, pltpu.roll(a, back_y, 0), aa, pltpu.roll(aa, back_y, 0))
            acc = acc + hy * (g - pltpu.roll(g, roll_y, 0))
            z = pl.ds(offs[i], NY)
            emit(j, i, x * keep_ref[n, z, :] + (jnp.exp2(arg[n, z, :]) - acc))


def flip(neg, count, i):
    return jnp.where(neg, count - 1 - i, i)


def load_natural(ref, index):
    return lambda o: ref[index, o * PER : (o + 1) * PER, :]


def store_tile(ref, index):
    def store(o, z, value):
        ref[index, o, z * NY : (z + 1) * NY, :] = value

    return store


def cut_kernel(info, x, h1, l1, copy, sems, out_sems):
    layers = copy.shape[0]
    neg = info[0] != 0
    base = jnp.where(neg, 0, layers - 2)
    order = [layers - 2, layers - 1, 0, *range(1, layers - 2)]
    places = [flip(neg, layers, j) for j in order]
    loads = [pltpu.make_async_copy(x.at[n], copy.at[n], sems.at[i]) for i, n in enumerate(places)]
    targets = [h1.at[places[0] - base], h1.at[places[1] - base], l1.at[0]]
    stores = [
        pltpu.make_async_copy(copy.at[places[i]], target, out_sems.at[i])
        for i, target in enumerate(targets)
    ]
    for load in loads:
        load.start()
    for load, store in zip(loads, stores):
        load.wait()
        store.start()
    for load in loads[3:]:
        load.wait()
    for store in stores:
        store.wait()


def start_kernel(info, x, raw, tab, tiles, mom, scale, h2, h3, l2, tmp, sems):
    layers, octants = tiles.shape[0], tiles.shape[1]
    neg, first = info[0] != 0, info[1]
    starts = [jnp.where(neg, 2, layers - 4), jnp.where(neg, 4, layers - 6), jnp.where(neg, layers - 3, 1)]
    copies = [
        pltpu.make_async_copy(x.at[pl.ds(begin, 2)], target, sems.at[i])
        for i, (begin, target) in enumerate(zip(starts, (h2, h3, l2)))
    ]
    for c in copies:
        c.start()

    @pl.loop(0, layers)
    def _(j):
        nat = flip(neg, layers, j)
        convert(load_natural(x, nat), store_tile(tiles, j), tmp, octants)

    for j in range(layers):
        nat = flip(neg, layers, j)
        total = 0.0
        for o in range(octants):
            total = total + moments_of(tiles[j, o], weight(tab, first + o))
        mom[nat] = total
    padded = jnp.concatenate([raw[0], jnp.zeros((LANES - layers, LANES), F32)], 0)
    tmp[0] = padded.T
    mixed = jnp.concatenate([tmp[0, pl.ds(z, NY, stride=NZ), :] for z in range(NZ)], 0).T
    for n in range(layers):
        scale[n] = mixed[n : n + 1]
    for c in copies:
        c.wait()


def share_kernel(ma, mb, scale, out):
    row = lax.broadcasted_iota(jnp.int32, (8, LANES), 0)
    for n in range(ma.shape[0]):
        out[n] = jnp.where(row == 5, scale[n], ma[n] + mb[n])


def first_kernel(info, tiles, h1, l1, ma, mb, scale, *refs):
    tab = refs[0]
    new, side, mom, tmp, arg, keep, carry = refs[1:]
    layers, octants = tiles.shape[0], tiles.shape[1]
    neg, first = info[0] != 0, info[1]
    for i in range(2):
        convert(load_natural(h1, flip(neg, 2, i)), store_tile(side, i), tmp, octants)
    convert(load_natural(l1, 0), store_tile(side, 2), tmp, octants)
    js = list(range(layers))
    co = {}
    for j in js:
        nat = flip(neg, layers, j)
        co[j] = coefficients(ma[nat] + mb[nat], scale[nat])
        mom[nat] = jnp.zeros((8, LANES), F32)
    prepare(js, co, tab, keep)
    outer = {-2: 0, -1: 1, layers: 2}

    def get(j):
        return (side, outer[j]) if j in outer else (tiles, j)

    @pl.loop(0, octants)
    def _(o):
        octant = first + o
        place = place_octant(octant)

        def emit(j, i, value):
            new[j, o, pl.ds(place[1][i], NY), :] = value

        advance(js, get, o, octant, place, co, tab, arg, keep, carry, emit)
        for j in js:
            mom[flip(neg, layers, j)] += moments_of(new[j, o], weight(tab, octant))


def edge_kernel(info, tiles, side, h2, l2, up_share, down_share, *refs):
    tab = refs[0]
    edge, far, mom, tmp, arg, keep, carry, below = refs[1:]
    layers, octants = tiles.shape[0], tiles.shape[1]
    neg, first = info[0] != 0, info[1]
    for i in range(2):
        convert(load_natural(h2, flip(neg, 2, i)), store_tile(far, i), tmp, octants)
        convert(load_natural(l2, flip(neg, 2, i)), store_tile(below, i), tmp, octants)
    up, down = [-2, -1], [layers, layers + 1]
    outer = {-2: 0, -1: 1, layers: 2, layers + 1: 3}
    co = {}
    for j in outer:
        if j < 0:
            known = up_share[flip(neg, layers, layers + j)]
        else:
            known = down_share[flip(neg, layers, j - layers)]
        co[j] = coefficients(known, known[5:6])
    prepare(up + down, co, tab, keep)
    for n in range(4):
        mom[n] = jnp.zeros((8, LANES), F32)

    def get(j):
        if j < -2:
            return far, j + 4
        if j < 0:
            return side, j + 2
        if j > layers:
            return below, j - layers - 1
        return (side, 2) if j == layers else (tiles, j)

    @pl.loop(0, octants)
    def _(o):
        octant = first + o
        place = place_octant(octant)

        def emit(j, i, value):
            edge[outer[j], o, pl.ds(place[1][i], NY), :] = value

        advance(up, get, o, octant, place, co, tab, arg, keep, carry, emit)
        advance(down, get, o, octant, place, co, tab, arg.at[2:], keep.at[2:], carry, emit)
        for n in range(4):
            mom[flip(neg, 4, n)] += moments_of(edge[n, o], weight(tab, octant))


def middle_kernel(info, new, ma, mb, scale, *refs):
    tab = refs[0]
    newer, mom, _, arg, keep, carry = refs[1:]
    layers, octants = new.shape[0], new.shape[1]
    neg, first = info[0] != 0, info[1]
    js = list(range(2, layers - 1))
    co = {}
    for j in js:
        nat = flip(neg, layers, j)
        co[j] = coefficients(ma[nat] + mb[nat], scale[nat])
        mom[j - 2] = jnp.zeros((8, LANES), F32)
    prepare(js, co, tab, keep)

    @pl.loop(0, octants)
    def _(o):
        octant = first + o
        place = place_octant(octant)

        def emit(j, i, value):
            newer[j - 2, o, pl.ds(place[1][i], NY), :] = value

        advance(js, lambda j: (new, j), o, octant, place, co, tab, arg, keep, carry, emit)
        for j in js:
            mom[j - 2] += moments_of(newer[j - 2, o], weight(tab, octant))


def second_kernel(info, new, edge, ma, mb, middle, scale, *refs):
    tab = refs[0]
    newer, mom, _, arg, keep, carry = refs[1:]
    layers, octants = new.shape[0], new.shape[1]
    neg, first = info[0] != 0, info[1]
    up, down = [0, 1], [layers - 1]
    slots = {0: 0, 1: 1, layers - 1: 2}
    co = {}
    for j in slots:
        nat = flip(neg, layers, j)
        co[j] = coefficients(ma[nat] + mb[nat], scale[nat])
        mom[nat] = jnp.zeros((8, LANES), F32)
    for j in range(2, layers - 1):
        mom[flip(neg, layers, j)] = middle[j - 2]
    prepare(up + down, co, tab, keep)
    outer = {-2: 0, -1: 1, layers: 2}

    def get(j):
        return (edge, outer[j]) if j in outer else (new, j)

    @pl.loop(0, octants)
    def _(o):
        octant = first + o
        place = place_octant(octant)

        def emit(j, i, value):
            newer[slots[j], o, pl.ds(place[1][i], NY), :] = value

        advance(up, get, o, octant, place, co, tab, arg, keep, carry, emit)
        advance(down, get, o, octant, place, co, tab, arg.at[2:], keep.at[2:], carry, emit)
        for j, n in slots.items():
            mom[flip(neg, layers, j)] += moments_of(newer[n, o], weight(tab, octant))


def third_kernel(info, side, far, h3, edge, new, ma, mb, up_share, down_share, *refs):
    tab = refs[0]
    beside, tmp, arg, keep, carry, last, rim = refs[1:]
    layers, octants = new.shape[0], new.shape[1]
    neg, first = info[0] != 0, info[1]
    for i in range(2):
        convert(load_natural(h3, flip(neg, 2, i)), store_tile(last, i), tmp, octants)
    js, up, down = [-4, -3], [-2, -1], [layers]
    outer = {-2: 0, -1: 1, layers: 2, layers + 1: 3}
    co = {}
    for j in js:
        known = up_share[flip(neg, layers, layers + j)]
        co[j] = coefficients(known, known[5:6])
    for i, j in enumerate(up + down):
        slot = flip(neg, 4, i)
        beyond = up_share[flip(neg, layers, layers + j)] if j < 0 else down_share[flip(neg, layers, 0)]
        co[j] = coefficients(ma[slot] + mb[slot], beyond[5:6])
    prepare(js + up + down, co, tab, keep)

    def get0(j):
        return (last, j + 6) if j < -4 else (far, j + 4) if j < -2 else (side, j + 2)

    def get1(j):
        return (rim, j + 4) if j < -2 else (edge, outer[j]) if j in outer else (new, j)

    @pl.loop(0, octants)
    def _(o):
        octant = first + o
        place = place_octant(octant)

        def emit1(j, i, value):
            rim[j + 4, o, pl.ds(place[1][i], NY), :] = value

        def emit2(j, i, value):
            beside[outer[j], o, pl.ds(place[1][i], NY), :] = value

        advance(down, get1, o, octant, place, co, tab, arg.at[4:], keep.at[4:], carry, emit2)
        advance(js, get0, o, octant, place, co, tab, arg, keep, carry, emit1)
        advance(up, get1, o, octant, place, co, tab, arg.at[2:], keep.at[2:], carry, emit2)


def last_kernel(info, middle, newer, beside, ma, mb, scale, *refs):
    tab = refs[0]
    out, _, arg, keep, carry, result, ready, sems = refs[1:]
    layers, octants = out.shape[0], newer.shape[1]
    neg, first = info[0] != 0, info[1]
    js = list(range(layers))
    outer = {-2: 0, -1: 1, layers: 2}
    slots = {0: 0, 1: 1, layers - 1: 2}
    co = {}
    for j in js:
        nat = flip(neg, layers, j)
        co[j] = coefficients(ma[nat] + mb[nat], scale[nat])
    prepare(js, co, tab, keep)

    def get(j):
        if j in outer:
            return beside, outer[j]
        return (newer, slots[j]) if j in slots else (middle, j - 2)

    @pl.loop(0, octants)
    def _(o):
        octant = first + o
        place = place_octant(octant)
        starts = [place[1][i] // NY for i in range(NZ)]

        def emit(j, i, value):
            result[j, o, pl.ds(starts[i], NY, stride=NZ), :] = value

        advance(js, get, o, octant, place, co, tab, arg, keep, carry, emit)

    copies = []
    for j in js:
        for o in range(octants):
            ready[j, o * PER : (o + 1) * PER, :] = result[j, o].T[:PER]
        copies.append(pltpu.make_async_copy(ready.at[j], out.at[flip(neg, layers, j)], sems.at[j]))
        copies[j].start()
    for c in copies:
        c.wait()


def scratch(octants, layers, extra=()):
    square = (LANES, LANES)
    return [
        pltpu.VMEM((octants, *square), F32),
        pltpu.VMEM((layers, *square), F32),
        pltpu.VMEM((layers, *square), F32),
        pltpu.VMEM((3, *square), F32),
        *extra,
    ]


def run(body, args, outs, scratch_shapes, far_args=(), far_outs=()):
    call = pl.pallas_call(
        body,
        out_shape=[
            pltpu.HBM(shape, F32) if i in far_outs else jax.ShapeDtypeStruct(shape, F32)
            for i, shape in enumerate(outs)
        ],
        in_specs=[
            SMEM if a.dtype == jnp.int32 else HBM if i in far_args else VMEM for i, a in enumerate(args)
        ],
        out_specs=[HBM if i in far_outs else VMEM for i in range(len(outs))],
        scratch_shapes=scratch_shapes,
        compiler_params=pltpu.CompilerParams(vmem_limit_bytes=24 * 2**20),
    )
    args = [
        pltpu.with_memory_space_constraint(a, pltpu.HBM) if i in far_args else a
        for i, a in enumerate(args)
    ]
    return call(*args)


def exchange(part, axis):
    count = lax.axis_size(axis)
    if count == 1:
        return part, jnp.zeros_like(part)
    if count & (count - 1):
        return lax.psum(part, axis), jnp.zeros_like(part)
    bit = 1
    while True:
        other = lax.ppermute(part, axis, [(i, i ^ bit) for i in range(count)])
        bit *= 2
        if bit == count:
            return part, other
        part = part + other


def body(distribution, collision_scale):
    vel_count, layers, _ = distribution.shape
    oct_count, ring = lax.axis_size("oct"), lax.axis_size("space")
    octants = vel_count // PER
    assert vel_count % PER == 0 and oct_count % 2 == 0 and layers >= 6
    first = lax.axis_index("oct") * octants
    neg = first // 4 % 2
    info = jnp.stack([neg, first]).astype(jnp.int32)
    toward = []
    for o in range(oct_count):
        step = -1 if o * octants // 4 % 2 else 1
        for s in range(ring):
            toward.append((o * ring + s, o * ring + (s + step) % ring))
    against = [(target, source) for source, target in toward]

    def send(block, pairs):
        return lax.ppermute(block, ("oct", "space"), pairs)

    x = jnp.transpose(distribution, (1, 0, 2))
    tab = table()
    tile = (octants, LANES, LANES)
    rows = (8, LANES)
    block = (2, vel_count, LANES)
    two, six = pltpu.VMEM((2, *tile), F32), pltpu.VMEM((layers, *tile), F32)
    dma = pltpu.SemaphoreType.DMA
    h1, l1, x = run(
        cut_kernel,
        (info, x),
        [block, (1, vel_count, LANES), (layers, vel_count, LANES)],
        [dma((layers,)), dma((3,))],
        far_args=(1,),
        far_outs=(0, 1),
    )
    h1, l1 = send(h1, toward), send(l1, against)
    tiles, m0, scale, h2, h3, l2 = run(
        start_kernel,
        (info, x, collision_scale, tab),
        [(layers, *tile), (layers, *rows), (layers, 1, LANES), block, block, block],
        [pltpu.VMEM(tile, F32), dma((3,))],
        far_outs=(3, 4, 5),
    )
    m0 = exchange(m0, "oct")
    h2, h3, l2 = send(h2, toward), send(h3, toward), send(l2, against)
    (share,) = run(share_kernel, (*m0, scale), [(layers, *rows)], [])
    ch, cl = send(share, toward), send(share, against)
    new, side, m1 = run(
        first_kernel,
        (info, tiles, h1, l1, *m0, scale, tab),
        [(layers, *tile), (3, *tile), (layers, *rows)],
        scratch(octants, layers),
    )
    m1 = exchange(m1, "oct")
    edge, far, medge = run(
        edge_kernel,
        (info, tiles, side, h2, l2, ch, cl, tab),
        [(4, *tile), (2, *tile), (4, *rows)],
        scratch(octants, 4, [two]),
    )
    medge = exchange(medge, "oct")
    middle, mm = run(
        middle_kernel,
        (info, new, *m1, scale, tab),
        [(layers - 3, *tile), (layers - 3, *rows)],
        scratch(octants, layers - 3),
    )
    newer, m2 = run(
        second_kernel,
        (info, new, edge, *m1, mm, scale, tab),
        [(3, *tile), (layers, *rows)],
        scratch(octants, 3),
    )
    m2 = exchange(m2, "oct")
    (beside,) = run(
        third_kernel,
        (info, side, far, h3, edge, new, *medge, ch, cl, tab),
        [(3, *tile)],
        scratch(octants, 5, [two, two]),
    )
    (out,) = run(
        last_kernel,
        (info, middle, newer, beside, *m2, scale, tab),
        [(layers, vel_count, LANES)],
        scratch(
            octants, layers, [six, pltpu.VMEM((layers, vel_count, LANES), F32), dma((layers,))]
        ),
        far_outs=(0,),
    )
    return jnp.transpose(out, (1, 0, 2))


def solution(mesh):
    return jax.shard_map(
        body,
        mesh=mesh,
        in_specs=(P("oct", "space", None), P(None, "space", None)),
        out_specs=P("oct", "space", None),
        check_vma=False,
    )
```

```python
import math

import jax
import jax.numpy as jnp
import numpy as np
from jax import lax
from jax.experimental import pallas as pl
from jax.experimental.pallas import tpu as pltpu
from jax.sharding import PartitionSpec as P


NV = 10
NZ = 16
NY = 8
HALF = NV // 2
PER = HALF**3
LANES = 128

vel_bound = 4.0
courant = 0.08
time_step = 0.08
base_rate = 0.25
visc_index = 0.81
limiter_eps = 0.01
spacing = 2.0 * vel_bound / NV
quad = spacing**3 * (2.0 * math.pi) ** (-1.5)
unit = 0.5 * spacing
log2e = math.log2(math.e)

VMEM = pl.BlockSpec(memory_space=pltpu.VMEM)
HBM = pl.BlockSpec(memory_space=pltpu.HBM)
SMEM = pl.BlockSpec(memory_space=pltpu.SMEM)
NT = (((1,), (1,)), ((), ()))
TN = (((0,), (0,)), ((), ()))
F32 = jnp.float32
BF16 = jnp.bfloat16


def table():
    within = np.arange(PER)
    size = np.stack([within // HALF**2, within // HALF % HALF, within % HALF]) * 2 + 1
    feature = np.zeros((9, 8, LANES), np.float32)
    for octant in range(8):
        sign = np.array([1 - 2 * (octant >> 2 & 1), 1 - 2 * (octant >> 1 & 1), 1 - 2 * (octant & 1)])
        feature[octant, 0, :PER] = 1
        feature[octant, 1:4, :PER] = size * sign[:, None]
        feature[octant, 4, :PER] = (size * size).sum(0)
    feature[8, 5] = 1
    pad = np.zeros_like(feature)
    return jnp.asarray(np.concatenate([feature, feature, feature, pad, feature, pad], axis=1), BF16)


def phi(tab, octant):
    return tab[octant, 0:32]


def weight(tab, octant):
    return tab[octant, 32:48]


def slope(left, right, left_sq, right_sq):
    return (left * right) * (left + right) * (1.0 / (left_sq + right_sq))


def place_octant(octant):
    pos_y = octant // 2 % 2 == 0
    pos_z = octant % 2 == 0
    roll_y = jnp.where(pos_y, 1, NY - 1)
    first = jnp.where(pos_z, 0, (NZ - 1) * NY)
    pace = jnp.where(pos_z, NY, -NY)
    offs = [pl.multiple_of(first + i * pace, NY) for i in range(NZ)]
    return roll_y, offs


def convert(load, store, tmp, octants):
    for o in range(octants):
        x = load(o)
        x = jnp.concatenate([x, jnp.zeros((LANES - PER, LANES), F32)], 0)
        tmp[o] = x.T
        for z in range(NZ):
            store(o, z, tmp[o, pl.ds(z, NY, stride=NZ), :])


def coefficients(total, scale):
    m0 = total[0:1]
    inv = 1.0 / m0
    ux = unit * total[1:2] * inv
    uy = unit * total[2:3] * inv
    uz = unit * total[3:4] * inv
    square = ux * ux + uy * uy + uz * uz
    temper = (unit * unit * total[4:5] * inv - square) * (1.0 / 3.0)
    log_t = jnp.log2(temper)
    density = quad * m0
    pace = (time_step * base_rate) * scale * density
    keep = 1.0 - pace * jnp.exp2((1.0 - visc_index) * log_t)
    beta = log2e / temper
    c0 = jnp.log2(pace * density) + (1.0 - visc_index - 1.5) * log_t - 0.5 * beta * square
    slow = unit * beta
    row = lax.broadcasted_iota(jnp.int32, (8, LANES), 0)
    c = jnp.where(row == 0, c0, 0.0)
    c = jnp.where(row == 1, slow * ux, c)
    c = jnp.where(row == 2, slow * uy, c)
    c = jnp.where(row == 3, slow * uz, c)
    c = jnp.where(row == 4, (-0.5 * unit) * slow, c)
    c = jnp.where(row == 5, keep, c)
    high = c.astype(BF16).astype(F32)
    rest = c - high
    middle = rest.astype(BF16).astype(F32)
    low = rest - middle
    return jnp.concatenate([high, middle, low, jnp.zeros_like(c)], 0).astype(BF16)


def moments_of(x, rows):
    high = x.astype(BF16)
    low = (x - high.astype(F32)).astype(BF16)
    m = lax.dot_general(rows, high, NT, preferred_element_type=F32)
    m = m + lax.dot_general(rows, low, NT, preferred_element_type=F32)
    return m[:8]


def prepare(js, coef, tab, keep_ref):
    for n, j in enumerate(js):
        keep_ref[n] = lax.dot_general(coef[j], phi(tab, 8), TN, preferred_element_type=F32)


def advance(js, get, o, octant, place, coef, tab, arg, keep_ref, carry, emit):
    roll_y, offs = place
    back_y = NY - roll_y
    half = (0.5 * courant * unit) * jnp.abs(weight(tab, octant).astype(F32))
    hx, hy, hz = half[1:2], half[2:3], half[3:4]
    for n, j in enumerate(js):
        arg[n] = lax.dot_general(coef[j], phi(tab, octant), TN, preferred_element_type=F32)

    def rd(j, i):
        ref, index = get(j)
        return ref[index, o, pl.ds(offs[i % NZ], NY), :]

    def square(d, index):
        return d * d + limiter_eps if index % 2 == 0 else d * d

    j = js[0] - 1
    for i in range(NZ):
        x = rd(j, i)
        a = x - rd(j - 1, i)
        b = rd(j + 1, i) - x
        bb = square(b, j)
        s = pl.ds(i * NY, NY)
        carry[0, s, :] = (x + x) + slope(a, b, square(a, j - 1), bb)
        carry[1, s, :] = b
        carry[2, s, :] = bb
    for n, j in enumerate(js):
        xm2, xm1, x0 = rd(j, NZ - 2), rd(j, NZ - 1), rd(j, 0)
        am, az = xm1 - xm2, x0 - xm1
        ez = square(az, NZ - 1)
        gz = (xm1 + xm1) + slope(am, az, square(am, NZ - 2), ez)
        for i in range(NZ):
            s = pl.ds(i * NY, NY)
            x, xn = x0, rd(j, i + 1)
            x2 = x + x
            an = xn - x
            en = square(an, i)
            gn = x2 + slope(az, an, ez, en)
            acc = hz * (gn - gz)
            az, ez, gz, x0 = an, en, gn, xn
            b = rd(j + 1, i) - x
            bb = square(b, j)
            g = x2 + slope(carry[1, s, :], b, carry[2, s, :], bb)
            acc = acc + hx * (g - carry[0, s, :])
            carry[0, s, :] = g
            carry[1, s, :] = b
            carry[2, s, :] = bb
            a = x - pltpu.roll(x, roll_y, 0)
            aa = a * a + 0.5 * limiter_eps
            g = x2 + slope(a, pltpu.roll(a, back_y, 0), aa, pltpu.roll(aa, back_y, 0))
            acc = acc + hy * (g - pltpu.roll(g, roll_y, 0))
            z = pl.ds(offs[i], NY)
            emit(j, i, x * keep_ref[n, z, :] + (jnp.exp2(arg[n, z, :]) - acc))


def flip(neg, count, i):
    return jnp.where(neg, count - 1 - i, i)


def load_natural(ref, index):
    return lambda o: ref[index, o * PER : (o + 1) * PER, :]


def store_tile(ref, index):
    def store(o, z, value):
        ref[index, o, z * NY : (z + 1) * NY, :] = value

    return store


def cut_kernel(info, x, h1, l1, copy, sems, out_sems):
    layers = copy.shape[0]
    neg = info[0] != 0
    base = jnp.where(neg, 0, layers - 2)
    order = [layers - 2, layers - 1, 0, *range(1, layers - 2)]
    places = [flip(neg, layers, j) for j in order]
    loads = [pltpu.make_async_copy(x.at[n], copy.at[n], sems.at[i]) for i, n in enumerate(places)]
    targets = [h1.at[places[0] - base], h1.at[places[1] - base], l1.at[0]]
    stores = [
        pltpu.make_async_copy(copy.at[places[i]], target, out_sems.at[i])
        for i, target in enumerate(targets)
    ]
    for load in loads:
        load.start()
    for load, store in zip(loads, stores):
        load.wait()
        store.start()
    for load in loads[3:]:
        load.wait()
    for store in stores:
        store.wait()


def start_kernel(info, x, raw, tab, tiles, mom, scale, h2, h3, l2, tmp, sems):
    layers, octants = tiles.shape[0], tiles.shape[1]
    neg, first = info[0] != 0, info[1]
    starts = [jnp.where(neg, 2, layers - 4), jnp.where(neg, 4, layers - 6), jnp.where(neg, layers - 3, 1)]
    copies = [
        pltpu.make_async_copy(x.at[pl.ds(begin, 2)], target, sems.at[i])
        for i, (begin, target) in enumerate(zip(starts, (h2, h3, l2)))
    ]
    for c in copies:
        c.start()

    @pl.loop(0, layers)
    def _(j):
        nat = flip(neg, layers, j)
        convert(load_natural(x, nat), store_tile(tiles, j), tmp, octants)

    for j in range(layers):
        nat = flip(neg, layers, j)
        total = 0.0
        for o in range(octants):
            total = total + moments_of(tiles[j, o], weight(tab, first + o))
        mom[nat] = total
    padded = jnp.concatenate([raw[0], jnp.zeros((LANES - layers, LANES), F32)], 0)
    tmp[0] = padded.T
    mixed = jnp.concatenate([tmp[0, pl.ds(z, NY, stride=NZ), :] for z in range(NZ)], 0).T
    for n in range(layers):
        scale[n] = mixed[n : n + 1]
    for c in copies:
        c.wait()


def share_kernel(ma, mb, scale, out):
    row = lax.broadcasted_iota(jnp.int32, (8, LANES), 0)
    for n in range(ma.shape[0]):
        out[n] = jnp.where(row == 5, scale[n], ma[n] + mb[n])


def first_kernel(info, tiles, h1, l1, ma, mb, scale, *refs):
    tab = refs[0]
    new, side, mom, tmp, arg, keep, carry = refs[1:]
    layers, octants = tiles.shape[0], tiles.shape[1]
    neg, first = info[0] != 0, info[1]
    for i in range(2):
        convert(load_natural(h1, flip(neg, 2, i)), store_tile(side, i), tmp, octants)
    convert(load_natural(l1, 0), store_tile(side, 2), tmp, octants)
    js = list(range(layers))
    co = {}
    for j in js:
        nat = flip(neg, layers, j)
        co[j] = coefficients(ma[nat] + mb[nat], scale[nat])
        mom[nat] = jnp.zeros((8, LANES), F32)
    prepare(js, co, tab, keep)
    outer = {-2: 0, -1: 1, layers: 2}

    def get(j):
        return (side, outer[j]) if j in outer else (tiles, j)

    @pl.loop(0, octants, unroll=min(2, octants))
    def _(o):
        octant = first + o
        place = place_octant(octant)

        def emit(j, i, value):
            new[j, o, pl.ds(place[1][i], NY), :] = value

        advance(js, get, o, octant, place, co, tab, arg, keep, carry, emit)
        for j in js:
            mom[flip(neg, layers, j)] += moments_of(new[j, o], weight(tab, octant))


def edge_kernel(info, tiles, side, h2, l2, up_share, down_share, *refs):
    tab = refs[0]
    edge, far, mom, tmp, arg, keep, carry, below = refs[1:]
    layers, octants = tiles.shape[0], tiles.shape[1]
    neg, first = info[0] != 0, info[1]
    for i in range(2):
        convert(load_natural(h2, flip(neg, 2, i)), store_tile(far, i), tmp, octants)
        convert(load_natural(l2, flip(neg, 2, i)), store_tile(below, i), tmp, octants)
    up, down = [-2, -1], [layers, layers + 1]
    outer = {-2: 0, -1: 1, layers: 2, layers + 1: 3}
    co = {}
    for j in outer:
        if j < 0:
            known = up_share[flip(neg, layers, layers + j)]
        else:
            known = down_share[flip(neg, layers, j - layers)]
        co[j] = coefficients(known, known[5:6])
    prepare(up + down, co, tab, keep)
    for n in range(4):
        mom[n] = jnp.zeros((8, LANES), F32)

    def get(j):
        if j < -2:
            return far, j + 4
        if j < 0:
            return side, j + 2
        if j > layers:
            return below, j - layers - 1
        return (side, 2) if j == layers else (tiles, j)

    @pl.loop(0, octants, unroll=min(2, octants))
    def _(o):
        octant = first + o
        place = place_octant(octant)

        def emit(j, i, value):
            edge[outer[j], o, pl.ds(place[1][i], NY), :] = value

        advance(up, get, o, octant, place, co, tab, arg, keep, carry, emit)
        advance(down, get, o, octant, place, co, tab, arg.at[2:], keep.at[2:], carry, emit)
        for n in range(4):
            mom[flip(neg, 4, n)] += moments_of(edge[n, o], weight(tab, octant))


def middle_kernel(info, new, ma, mb, scale, *refs):
    tab = refs[0]
    newer, mom, _, arg, keep, carry = refs[1:]
    layers, octants = new.shape[0], new.shape[1]
    neg, first = info[0] != 0, info[1]
    js = list(range(2, layers - 1))
    co = {}
    for j in js:
        nat = flip(neg, layers, j)
        co[j] = coefficients(ma[nat] + mb[nat], scale[nat])
        mom[j - 2] = jnp.zeros((8, LANES), F32)
    prepare(js, co, tab, keep)

    @pl.loop(0, octants, unroll=min(2, octants))
    def _(o):
        octant = first + o
        place = place_octant(octant)

        def emit(j, i, value):
            newer[j - 2, o, pl.ds(place[1][i], NY), :] = value

        advance(js, lambda j: (new, j), o, octant, place, co, tab, arg, keep, carry, emit)
        for j in js:
            mom[j - 2] += moments_of(newer[j - 2, o], weight(tab, octant))


def second_kernel(info, new, edge, ma, mb, middle, scale, *refs):
    tab = refs[0]
    newer, mom, _, arg, keep, carry = refs[1:]
    layers, octants = new.shape[0], new.shape[1]
    neg, first = info[0] != 0, info[1]
    up, down = [0, 1], [layers - 1]
    slots = {0: 0, 1: 1, layers - 1: 2}
    co = {}
    for j in slots:
        nat = flip(neg, layers, j)
        co[j] = coefficients(ma[nat] + mb[nat], scale[nat])
        mom[nat] = jnp.zeros((8, LANES), F32)
    for j in range(2, layers - 1):
        mom[flip(neg, layers, j)] = middle[j - 2]
    prepare(up + down, co, tab, keep)
    outer = {-2: 0, -1: 1, layers: 2}

    def get(j):
        return (edge, outer[j]) if j in outer else (new, j)

    @pl.loop(0, octants, unroll=min(2, octants))
    def _(o):
        octant = first + o
        place = place_octant(octant)

        def emit(j, i, value):
            newer[slots[j], o, pl.ds(place[1][i], NY), :] = value

        advance(up, get, o, octant, place, co, tab, arg, keep, carry, emit)
        advance(down, get, o, octant, place, co, tab, arg.at[2:], keep.at[2:], carry, emit)
        for j, n in slots.items():
            mom[flip(neg, layers, j)] += moments_of(newer[n, o], weight(tab, octant))


def third_kernel(info, side, far, h3, edge, new, ma, mb, up_share, down_share, *refs):
    tab = refs[0]
    beside, tmp, arg, keep, carry, last, rim = refs[1:]
    layers, octants = new.shape[0], new.shape[1]
    neg, first = info[0] != 0, info[1]
    for i in range(2):
        convert(load_natural(h3, flip(neg, 2, i)), store_tile(last, i), tmp, octants)
    js, up, down = [-4, -3], [-2, -1], [layers]
    outer = {-2: 0, -1: 1, layers: 2, layers + 1: 3}
    co = {}
    for j in js:
        known = up_share[flip(neg, layers, layers + j)]
        co[j] = coefficients(known, known[5:6])
    for i, j in enumerate(up + down):
        slot = flip(neg, 4, i)
        beyond = up_share[flip(neg, layers, layers + j)] if j < 0 else down_share[flip(neg, layers, 0)]
        co[j] = coefficients(ma[slot] + mb[slot], beyond[5:6])
    prepare(js + up + down, co, tab, keep)

    def get0(j):
        return (last, j + 6) if j < -4 else (far, j + 4) if j < -2 else (side, j + 2)

    def get1(j):
        return (rim, j + 4) if j < -2 else (edge, outer[j]) if j in outer else (new, j)

    @pl.loop(0, octants, unroll=min(2, octants))
    def _(o):
        octant = first + o
        place = place_octant(octant)

        def emit1(j, i, value):
            rim[j + 4, o, pl.ds(place[1][i], NY), :] = value

        def emit2(j, i, value):
            beside[outer[j], o, pl.ds(place[1][i], NY), :] = value

        advance(down, get1, o, octant, place, co, tab, arg.at[4:], keep.at[4:], carry, emit2)
        advance(js, get0, o, octant, place, co, tab, arg, keep, carry, emit1)
        advance(up, get1, o, octant, place, co, tab, arg.at[2:], keep.at[2:], carry, emit2)


def last_kernel(info, middle, newer, beside, ma, mb, scale, *refs):
    tab = refs[0]
    out, _, arg, keep, carry, result, ready, sems = refs[1:]
    layers, octants = out.shape[0], newer.shape[1]
    neg, first = info[0] != 0, info[1]
    js = list(range(layers))
    outer = {-2: 0, -1: 1, layers: 2}
    slots = {0: 0, 1: 1, layers - 1: 2}
    co = {}
    for j in js:
        nat = flip(neg, layers, j)
        co[j] = coefficients(ma[nat] + mb[nat], scale[nat])
    prepare(js, co, tab, keep)

    def get(j):
        if j in outer:
            return beside, outer[j]
        return (newer, slots[j]) if j in slots else (middle, j - 2)

    @pl.loop(0, octants, unroll=min(2, octants))
    def _(o):
        octant = first + o
        place = place_octant(octant)
        starts = [place[1][i] // NY for i in range(NZ)]

        def emit(j, i, value):
            result[j, o, pl.ds(starts[i], NY, stride=NZ), :] = value

        advance(js, get, o, octant, place, co, tab, arg, keep, carry, emit)

    copies = []
    for j in js:
        for o in range(octants):
            ready[j, o * PER : (o + 1) * PER, :] = result[j, o].T[:PER]
        copies.append(pltpu.make_async_copy(ready.at[j], out.at[flip(neg, layers, j)], sems.at[j]))
        copies[j].start()
    for c in copies:
        c.wait()


def scratch(octants, layers, extra=()):
    square = (LANES, LANES)
    return [
        pltpu.VMEM((octants, *square), F32),
        pltpu.VMEM((layers, *square), F32),
        pltpu.VMEM((layers, *square), F32),
        pltpu.VMEM((3, *square), F32),
        *extra,
    ]


def run(body, args, outs, scratch_shapes, far_args=(), far_outs=()):
    call = pl.pallas_call(
        body,
        out_shape=[
            pltpu.HBM(shape, F32) if i in far_outs else jax.ShapeDtypeStruct(shape, F32)
            for i, shape in enumerate(outs)
        ],
        in_specs=[
            SMEM if a.dtype == jnp.int32 else HBM if i in far_args else VMEM for i, a in enumerate(args)
        ],
        out_specs=[HBM if i in far_outs else VMEM for i in range(len(outs))],
        scratch_shapes=scratch_shapes,
        compiler_params=pltpu.CompilerParams(vmem_limit_bytes=24 * 2**20),
    )
    args = [
        pltpu.with_memory_space_constraint(a, pltpu.HBM) if i in far_args else a
        for i, a in enumerate(args)
    ]
    return call(*args)


def exchange(part, axis):
    count = lax.axis_size(axis)
    if count == 1:
        return part, jnp.zeros_like(part)
    if count & (count - 1):
        return lax.psum(part, axis), jnp.zeros_like(part)
    bit = 1
    while True:
        other = lax.ppermute(part, axis, [(i, i ^ bit) for i in range(count)])
        bit *= 2
        if bit == count:
            return part, other
        part = part + other


def body(distribution, collision_scale):
    vel_count, layers, _ = distribution.shape
    oct_count, ring = lax.axis_size("oct"), lax.axis_size("space")
    octants = vel_count // PER
    assert vel_count % PER == 0 and oct_count % 2 == 0 and layers >= 6
    first = lax.axis_index("oct") * octants
    neg = first // 4 % 2
    info = jnp.stack([neg, first]).astype(jnp.int32)
    toward = []
    for o in range(oct_count):
        step = -1 if o * octants // 4 % 2 else 1
        for s in range(ring):
            toward.append((o * ring + s, o * ring + (s + step) % ring))
    against = [(target, source) for source, target in toward]

    def send(block, pairs):
        return lax.ppermute(block, ("oct", "space"), pairs)

    x = jnp.transpose(distribution, (1, 0, 2))
    tab = table()
    tile = (octants, LANES, LANES)
    rows = (8, LANES)
    block = (2, vel_count, LANES)
    two, six = pltpu.VMEM((2, *tile), F32), pltpu.VMEM((layers, *tile), F32)
    dma = pltpu.SemaphoreType.DMA
    h1, l1, x = run(
        cut_kernel,
        (info, x),
        [block, (1, vel_count, LANES), (layers, vel_count, LANES)],
        [dma((layers,)), dma((3,))],
        far_args=(1,),
        far_outs=(0, 1),
    )
    h1, l1 = send(h1, toward), send(l1, against)
    tiles, m0, scale, h2, h3, l2 = run(
        start_kernel,
        (info, x, collision_scale, tab),
        [(layers, *tile), (layers, *rows), (layers, 1, LANES), block, block, block],
        [pltpu.VMEM(tile, F32), dma((3,))],
        far_outs=(3, 4, 5),
    )
    m0 = exchange(m0, "oct")
    h2, h3, l2 = send(h2, toward), send(h3, toward), send(l2, against)
    (share,) = run(share_kernel, (*m0, scale), [(layers, *rows)], [])
    ch, cl = send(share, toward), send(share, against)
    new, side, m1 = run(
        first_kernel,
        (info, tiles, h1, l1, *m0, scale, tab),
        [(layers, *tile), (3, *tile), (layers, *rows)],
        scratch(octants, layers),
    )
    m1 = exchange(m1, "oct")
    edge, far, medge = run(
        edge_kernel,
        (info, tiles, side, h2, l2, ch, cl, tab),
        [(4, *tile), (2, *tile), (4, *rows)],
        scratch(octants, 4, [two]),
    )
    medge = exchange(medge, "oct")
    middle, mm = run(
        middle_kernel,
        (info, new, *m1, scale, tab),
        [(layers - 3, *tile), (layers - 3, *rows)],
        scratch(octants, layers - 3),
    )
    newer, m2 = run(
        second_kernel,
        (info, new, edge, *m1, mm, scale, tab),
        [(3, *tile), (layers, *rows)],
        scratch(octants, 3),
    )
    m2 = exchange(m2, "oct")
    (beside,) = run(
        third_kernel,
        (info, side, far, h3, edge, new, *medge, ch, cl, tab),
        [(3, *tile)],
        scratch(octants, 5, [two, two]),
    )
    (out,) = run(
        last_kernel,
        (info, middle, newer, beside, *m2, scale, tab),
        [(layers, vel_count, LANES)],
        scratch(
            octants, layers, [six, pltpu.VMEM((layers, vel_count, LANES), F32), dma((layers,))]
        ),
        far_outs=(0,),
    )
    return jnp.transpose(out, (1, 0, 2))


def solution(mesh):
    return jax.shard_map(
        body,
        mesh=mesh,
        in_specs=(P("oct", "space", None), P(None, "space", None)),
        out_specs=P("oct", "space", None),
        check_vma=False,
    )
```
